1024 devices in a mesh: dp: 16 (over y, core), ep: 64 (over x, z).
Axes of the slice: x: 4, y: 8, z: 16, core: 2. Of those that a mesh axis runs over, the one named last changes fastest.
Arguments:
- expert_ids: int32 [16, 1024, 8], P('dp', 'ep'), may hold values from 0 to 63, all different within a row; in each aligned block of 16 rows (0 to 15, 16 to 31, ..., all dimensions but the last counted through in order) at most 4 rows name the same one
- route_weights: float32 [16, 1024, 8], P('dp', 'ep'), may hold values from 0.03 to 0.4
- saved_rows: bfloat16 [16, 64, 256, 2048], P('dp', 'ep'), may hold values from -6 to 6
- saved_gate_up: bfloat16 [16, 64, 256, 1536], P('dp', 'ep'), may hold values from -6 to 6
- hidden_grad: bfloat16 [16, 64, 256, 768], P('dp', 'ep'), may hold values from -6 to 6
- gate_up_weight: bfloat16 [64, 2048, 1536], P('ep'), may hold values from -0.125 to 0.125
Outputs:
- input_grad: bfloat16 [16, 1024, 2048], P('dp', 'ep')
- weight_grad: float32 [2048, 64, 1536], P('dp', 'ep')
The draws below stay inside these ranges and needn't reach their ends.
Inputs may be any that keep to these rules, and one draw needn't show every extreme that they name: `expert_ids`: each token names 8 different experts; among the tokens of one device no expert is named more than 4 times, a bound that some block reaches.
All inputs are finite; a program needn't handle non-finite values.
Results may differ from the reference program's by a relative error of at most 0.017.
Values may be sent and summed in bfloat16 or wider, within the bound.
No kernel may reach another device: no remote copies, remote signals or barrier semaphores. Data moves between devices by JAX's collectives and lax.ppermute only.
A program may use at most 64 MiB of HBM per device.

```python
import math
import jax
import jax.numpy as jnp
import numpy as np
from jax import lax

D = 2048
FF = 768
TOP = 8
TOK_DEV = 16
EXPERTS = 64
CAP = 4
SLOTS = 256
TOKENS = 1024
N_DP = 16
N_EP = 64


def with_spikes(values, rng, source, target, parts, factor):
    owner, partner = [(jnp.arange(values.shape[position]) // (values.shape[position] // parts)).reshape([-1 if axis == position else 1 for axis in range(values.ndim)]) for position in (source, target)]
    chosen = jax.random.permutation(rng, parts)[partner]
    strong = (owner == chosen) | (owner == (partner + parts // 2) % parts)
    return jnp.where(strong, factor * values, values)


def block_levels(stream_key, dims, pieces, low, top_value):
    def one(position, shards_of):
        draws = jax.random.uniform(jax.random.fold_in(jax.random.fold_in(stream_key, 6), position), (shards_of,), jnp.float32, low / len(pieces), top_value / len(pieces))
        return jnp.repeat(jnp.exp(draws), dims[position] // shards_of).reshape((-1,) + (1,) * (len(dims) - position - 1))

    level = one(*pieces[0])
    for cut in pieces[1:]:
        level = level * one(*cut)
    return level


def routed_block(own_key, own, number, rows, number_of, top, most, skew):
    ranking = jax.random.permutation(own_key, number_of)
    packed, common = shares(number_of, rows * top, most, skew, True), shares(number_of, rows * top, most, skew, False)
    places = jnp.arange(number_of)

    def named(lengths, rotation):
        used = int((lengths > 0).sum())
        fixed = max(1, used // 4)
        passed = fixed + (places - fixed + rotation * (used - fixed)) % max(1, number_of - fixed)
        return jnp.zeros((number_of,), jnp.int32).at[ranking[jnp.where(places < fixed, places, passed)]].set(jnp.asarray(lengths, jnp.int32))

    lengths = jnp.where(number % 4 == 0, named(packed, number // 4), named(common, number - number // 4 - 1))
    mixed = jax.random.permutation(jax.random.fold_in(own, 3), number_of)
    source_of, receiver = mixed[0:number_of // 2 * 2:2], mixed[1:number_of // 2 * 2:2]
    margin = jnp.minimum(lengths[source_of] - 1, most - lengths[receiver]) // 2
    margin = jnp.where((source_of == ranking[0]) | (receiver == ranking[0]) | (lengths[receiver] == 0), 0, jnp.maximum(margin, 0))
    passed = jax.random.randint(jax.random.fold_in(own, 4), (number_of // 2,), 0, 1 << 20) % (margin + 1)
    lengths = lengths.at[source_of].add(-passed).at[receiver].add(passed)
    members = jnp.searchsorted(jnp.cumsum(lengths), jnp.arange(rows * top), side="right").astype(jnp.int32)
    grid = members.reshape(top, rows).T
    grid = grid[jax.random.permutation(jax.random.fold_in(own, 1), rows)]
    rotation = jax.random.randint(jax.random.fold_in(own, 2), (rows, 1), 0, top)
    return jnp.take_along_axis(grid, (jnp.arange(top)[None, :] + rotation) % top, axis=1)


def shares(number_of, total, most, slope, full):
    portions = [(1 << 20) // math.isqrt(rank ** slope) + 1 for rank in range(1, number_of + 1)]
    largest = most if full else min(most, max(-(-total // number_of), total * portions[0] // sum(portions)))
    least = 1 if total - largest >= number_of - 1 else 0
    given, spare = [largest] + [least] * (number_of - 1), total - largest - least * (number_of - 1)
    while spare > 0:
        movable = [i for i in range(1, number_of) if given[i] < largest] or [i for i in range(1, number_of) if given[i] < most]
        mass, remaining = sum([portions[i] for i in movable]), spare
        for i in movable:
            extra = min(most - given[i], max(1, remaining * portions[i] // mass), spare)
            given[i] = given[i] + extra
            spare = spare - extra
    return np.array(given)


def normal_values(rng, dims, width, limit, cuts=(), kind=jnp.bfloat16):
    gain = block_levels(rng, dims, cuts, -0.22, 0.18) if cuts else 1.0
    array = jax.random.normal(rng, dims, jnp.float32) * width * gain
    return jnp.minimum(jnp.maximum(array, -limit), limit).astype(kind)


def heavy_noise(own_key, extent, deviation, bound, split, heavy, kind=jnp.bfloat16):
    drawn = deviation * jax.random.normal(own_key, extent, jnp.float32)
    if split:
        drawn = drawn * block_levels(own_key, extent, split, -0.22, 0.18)
    return jnp.clip(with_spikes(drawn, jax.random.fold_in(own_key, 3), *heavy), -bound, bound).astype(kind)


def setup_inputs(seed: int = 0) -> dict:
    streams_of = jax.random.split(jax.random.key(seed), 7)
    expert_ids_keys = jax.random.split(jax.random.fold_in(streams_of[0], 1), N_DP * TOKENS // TOK_DEV)
    expert_ids_turns = jax.random.permutation(jax.random.fold_in(streams_of[0], 3), N_DP * TOKENS // TOK_DEV)
    expert_ids = jax.vmap(lambda own, number: routed_block(jax.random.fold_in(streams_of[0], 2), own, number, TOK_DEV, EXPERTS, TOP, CAP, 2))(expert_ids_keys, expert_ids_turns).reshape((N_DP, TOKENS, TOP))
    route_weights = jnp.clip(jnp.exp(math.log(0.4) - 2.5902672 * jax.random.uniform(streams_of[1], (N_DP, TOKENS, TOP), jnp.float32) ** block_levels(streams_of[1], (N_DP, TOKENS, TOP), ((0, 16), (1, 64)), -0.2, 0.2)), 0.03, 0.4)
    saved_rows = heavy_noise(streams_of[2], (N_DP, EXPERTS, SLOTS, D), 1.0, 6.0, ((0, 16), (1, 64)), (0, 3, 16, 2.0))
    saved_gate_up = normal_values(streams_of[3], (N_DP, EXPERTS, SLOTS, 2 * FF), 1.5, 6.0, ((0, 16), (1, 64)))
    hidden_grad = normal_values(streams_of[4], (N_DP, EXPERTS, SLOTS, FF), 1.0, 6.0, ((0, 16), (1, 64)))
    gate_up_weight = normal_values(streams_of[5], (EXPERTS, D, 2 * FF), D ** -0.5, 0.125, ((0, 64),))
    return {"expert_ids": expert_ids, "route_weights": route_weights, "saved_rows": saved_rows, "saved_gate_up": saved_gate_up, "hidden_grad": hidden_grad, "gate_up_weight": gate_up_weight}


def route_tables(expert_ids):
    blocks = expert_ids.reshape(N_DP * N_EP, TOK_DEV * TOP)
    onehot = (blocks[:, :, None] == jnp.arange(EXPERTS, dtype=jnp.int32)[None, None, :]).astype(jnp.int32)
    before = (jnp.cumsum(onehot, axis=1) - onehot).astype(jnp.int32)
    rank_in_block = jnp.sum(before * onehot, axis=2).astype(jnp.int32).reshape(N_DP, TOKENS, TOP)
    counts = jnp.sum(onehot, axis=1).astype(jnp.int32).reshape(N_DP, N_EP, EXPERTS)
    return rank_in_block, counts


def reference(expert_ids, route_weights, saved_rows, saved_gate_up, hidden_grad, gate_up_weight):
    rank_in_block, counts = route_tables(expert_ids)
    per_expert = jnp.transpose(counts, (0, 2, 1))
    live_mask = (jnp.arange(CAP, dtype=jnp.int32)[None, None, None, :] < per_expert[..., None]).reshape(N_DP, EXPERTS, SLOTS)
    gate_pre = saved_gate_up[..., :FF].astype(jnp.float32)
    up_pre = saved_gate_up[..., FF:].astype(jnp.float32)
    grad_hidden = hidden_grad.astype(jnp.float32)
    sigma_gate = jax.nn.sigmoid(gate_pre)
    grad_gate = grad_hidden * up_pre * sigma_gate * (1.0 + gate_pre * (1.0 - sigma_gate))
    grad_up = grad_hidden * gate_pre * sigma_gate
    slot_grads = (jnp.concatenate([grad_gate, grad_up], axis=-1) * live_mask[..., None].astype(jnp.float32)).astype(jnp.bfloat16)

    def expert_work(index):
        rows = lax.dynamic_index_in_dim(saved_rows, index, 1, keepdims=False).astype(jnp.float32)
        grads = lax.dynamic_index_in_dim(slot_grads, index, 1, keepdims=False).astype(jnp.float32)
        weight = lax.dynamic_index_in_dim(gate_up_weight, index, 0, keepdims=False).astype(jnp.float32)
        row_grads = jnp.einsum('rsf,df->rsd', grads, weight).astype(jnp.bfloat16)
        partial_value = jnp.einsum('rsd,rsf->rdf', rows, grads)
        rounded = lax.optimization_barrier(partial_value.astype(jnp.bfloat16))
        summed = jnp.sum(rounded.astype(jnp.float32), axis=0) / N_DP
        return row_grads, summed

    row_grads, weight_sums = lax.map(expert_work, jnp.arange(EXPERTS, dtype=jnp.int32))
    replica_index = jnp.arange(N_DP, dtype=jnp.int32)[:, None, None]
    slot_index = ((jnp.arange(TOKENS, dtype=jnp.int32) // TOK_DEV)[None, :, None] * CAP + rank_in_block).astype(jnp.int32)
    picked = row_grads[expert_ids, replica_index, slot_index]
    combined = jnp.sum(route_weights[..., None] * picked.astype(jnp.float32), axis=2)
    input_grad = combined.astype(jnp.bfloat16)
    weight_grad = jnp.transpose(weight_sums, (1, 0, 2))
    return input_grad, weight_grad
```

```python
import functools
import jax
import jax.numpy as jnp
from jax import lax
from jax.experimental import pallas as pl
from jax.experimental.pallas import tpu as pltpu
from jax.sharding import PartitionSpec as P

ROWS_LIMIT = 60 << 20
BF16, F32, I32 = jnp.bfloat16, jnp.float32, jnp.int32


def dot(a, b, ca, cb):
    return lax.dot_general(a, b, (((ca,), (cb,)), ((), ())), preferred_element_type=F32)


def iota(shape, dim):
    return lax.broadcasted_iota(I32, shape, dim)


def cost(flops, nbytes):
    return pl.CostEstimate(flops=flops, bytes_accessed=nbytes, transcendentals=0)


def flatten_pairs(x_t):
    chosen, tokens = x_t.shape
    pairs = chosen * tokens
    pair = iota((chosen, pairs), 1)
    mine = pair % chosen == iota((chosen, pairs), 0)
    out = jnp.zeros((chosen, pairs), x_t.dtype)
    for t in range(tokens):
        out = jnp.where(mine & (pair // chosen == t), x_t[:, t : t + 1], out)
    return jnp.sum(out, axis=0, keepdims=True)


def route_kernel(ids_ref, cnt_ref, tgt_ref):
    experts = cnt_ref.shape[0]
    flat = flatten_pairs(ids_ref[...])
    pairs = flat.shape[1]
    onehot = (iota((experts, pairs), 0) == flat).astype(F32)
    upper = (iota((pairs, pairs), 0) < iota((pairs, pairs), 1)).astype(BF16)
    before = dot(onehot.astype(BF16), upper, 1, 0)
    rank = jnp.sum(before * onehot, axis=0, keepdims=True).astype(I32)
    tgt_ref[...] = flat * 8 + rank
    counts = jnp.sum(onehot, axis=1, keepdims=True).astype(I32)
    cnt_ref[:, 0, :] = jnp.broadcast_to(counts, (experts, cnt_ref.shape[2]))


def rows_kernel(me_ref, gu_ref, hg_ref, rows_ref, wlo_ref, whi_ref, trade_ref, out_ref, grads_ref):
    @pl.when(pl.program_id(0) == 0)
    def _():
        hidden = hg_ref.shape[1]
        gate = gu_ref[:, :hidden].astype(F32)
        up = gu_ref[:, hidden:].astype(F32)
        grad = hg_ref[...].astype(F32)
        sigma = jax.nn.sigmoid(gate)
        grads_ref[:, :hidden] = (grad * up * sigma * (1.0 + gate * (1.0 - sigma))).astype(BF16)
        grads_ref[:, hidden:] = (grad * gate * sigma).astype(BF16)
        part = trade_ref.shape[2]
        tiles = 2 * hidden // part
        for tile in range(tiles):
            trade_ref[tile] = grads_ref[:, tile * part : (tile + 1) * part]
        second = lax.rem(me_ref[0], 2) == 0
        for chunk in range(trade_ref.shape[0] - tiles):
            start = 2 * chunk * part
            trade_ref[tiles + chunk] = jnp.where(
                second,
                rows_ref[:, start + part : start + 2 * part],
                rows_ref[:, start : start + part],
            )

    grads = grads_ref[...]
    low = dot(grads, wlo_ref[...], 1, 1)
    high = dot(grads, whi_ref[...], 1, 1)
    slots, width = low.shape
    low = low.reshape(slots // 8, 8, width)
    high = high.reshape(slots // 8, 8, width)
    first = iota(low.shape, 1) < 4
    out_ref[:, 0] = jnp.where(first, low, pltpu.roll(high, 4, 1)).astype(BF16)
    out_ref[:, 1] = jnp.where(first, pltpu.roll(low, 4, 1), high).astype(BF16)


def live(cnt_ref, slots, part):
    experts = cnt_ref.shape[0]
    spread = (iota((slots, experts), 0) // 4 == iota((slots, experts), 1)).astype(BF16)
    counts = dot(spread, cnt_ref[...].astype(F32).astype(BF16), 1, 0)
    mask = (iota((slots, counts.shape[1]), 0) % 4).astype(F32) < counts
    return mask[:, :part]


def tiles_of(ref):
    return jnp.concatenate([ref[tile] for tile in range(ref.shape[0])], axis=1)


def partial_sum(cnt_a, cnt_b, rows_a, rows_b, grads_a, grads_b):
    slots, part = rows_a.shape
    zero = jnp.zeros((), F32)
    a = jnp.where(live(cnt_a, slots, part), rows_a[...].astype(F32), zero).astype(BF16)
    b = jnp.where(live(cnt_b, slots, part), rows_b[0].astype(F32), zero).astype(BF16)
    return dot(a, tiles_of(grads_a), 0, 0) + dot(b, tiles_of(grads_b), 0, 0)


def first_kernel(me_ref, *refs):
    refs[-1][...] = partial_sum(*refs[:6]).astype(BF16)


def second_kernel(side, me_ref, *refs):
    inc, out_ref = refs[6:]
    half = inc.shape[1]
    total = partial_sum(*refs[:6])
    low, high = total[:, :half], total[:, half:]
    if side == 0:
        low = low + inc[...].astype(F32)
    else:
        high = high + inc[...].astype(F32)
    out_ref[:, :half] = low.astype(BF16)
    out_ref[:, half:] = high.astype(BF16)


def middle_kernel(me_ref, *refs):
    inc, out_ref = refs[6:]
    out_ref[...] = (partial_sum(*refs[:6]) + inc[...].astype(F32)).astype(BF16)


def last_kernel(replicas, me_ref, *refs):
    one, two, out_ref = refs[6:]
    total = partial_sum(*refs[:6]) + (one[...].astype(F32) + two[...].astype(F32))
    out_ref[:, 0, :] = total / replicas


def spread_kernel(tgt_ref, w_ref, out_ref):
    _, double, rows = out_ref.shape
    tokens = double // 2
    pairs = tgt_ref.shape[1]
    chosen = pairs // tokens
    weight = flatten_pairs(w_ref[...])
    token_of = (iota((tokens, pairs), 1) // chosen == iota((tokens, pairs), 0)).astype(BF16)
    for side in range(2):
        hit = iota((rows, pairs), 0) == tgt_ref[...] + 4 * side
        spread = jnp.where(hit, weight, jnp.zeros((), F32))
        high = spread.astype(BF16)
        low = (spread - high.astype(F32)).astype(BF16)
        out_ref[side, :tokens] = dot(token_of, high, 1, 1).astype(BF16)
        out_ref[side, tokens:] = dot(token_of, low, 1, 1).astype(BF16)


def combine_kernel(spread_ref, recv_ref, out_ref):
    tokens, model = out_ref.shape
    recv = recv_ref[...]
    for side in range(2):
        both = dot(spread_ref[side], recv, 1, 0)
        out = both[:tokens] + both[tokens:]
        out_ref[:, side * (model // 2) : (side + 1) * (model // 2)] = out.astype(BF16)


def shards(ids, weights, rows, gate_up, hidden_grad, expert_weight, interpret=False):
    def call(body, limit=16 << 20, **options):
        params = pltpu.CompilerParams(vmem_limit_bytes=limit)
        return pl.pallas_call(body, interpret=interpret, compiler_params=params, **options)

    tokens, chosen = ids.shape[1:]
    slots, model = rows.shape[2:]
    hidden = hidden_grad.shape[3]
    wide = 2 * hidden
    experts = lax.axis_size("ep")
    replicas = lax.axis_size("dp")
    ring = replicas // 2
    part = model // replicas
    pairs = tokens * chosen
    rows = rows.reshape(slots, model)
    gate_up = gate_up.reshape(slots, wide)
    hidden_grad = hidden_grad.reshape(slots, hidden)
    expert_weight = expert_weight.reshape(model, wide)
    me = lax.axis_index("dp").astype(I32).reshape(1)
    sds = jax.ShapeDtypeStruct

    counts, target = call(
        route_kernel,
        out_shape=(sds((experts, 1, 128), I32), sds((1, pairs), I32)),
        name="route",
    )(ids.reshape(tokens, chosen).T)
    counts = lax.all_to_all(counts, "ep", split_axis=0, concat_axis=0, tiled=True)

    half = model // 2
    tile = min(256, half)
    steps = half // tile
    tiles = wide // part
    trade, sent = call(
        rows_kernel,
        limit=ROWS_LIMIT,
        grid_spec=pltpu.PrefetchScalarGridSpec(
            num_scalar_prefetch=1,
            grid=(steps,),
            in_specs=[
                pl.BlockSpec((slots, wide), lambda i, me: (0, 0)),
                pl.BlockSpec((slots, hidden), lambda i, me: (0, 0)),
                pl.BlockSpec((slots, model), lambda i, me: (0, 0)),
                pl.BlockSpec((tile, wide), lambda i, me: (i, 0)),
                pl.BlockSpec((tile, wide), lambda i, me: (i + steps, 0)),
            ],
            out_specs=(
                pl.BlockSpec((tiles + ring, slots, part), lambda i, me: (0, 0, 0)),
                pl.BlockSpec((slots // 8, 2, 8, tile), lambda i, me: (0, 0, 0, i)),
            ),
            scratch_shapes=[pltpu.VMEM((slots, wide), BF16)],
        ),
        out_shape=(
            sds((tiles + ring, slots, part), BF16),
            sds((slots // 8, 2, 8, half), BF16),
        ),
        cost_estimate=cost(2 * slots * model * wide, 2 * (model * wide + 4 * slots * wide)),
        name="rows",
    )(me, gate_up, hidden_grad, rows, expert_weight, expert_weight)
    returned = lax.all_to_all(
        sent.reshape(experts, 8, half), "ep", split_axis=0, concat_axis=0, tiled=True
    )

    def neighbour(d, direction):
        turn = direction if d % 2 == 0 else -direction
        return ((d // 2 + turn) % ring) * 2 + d % 2

    partner = [(d, d ^ 1) for d in range(replicas)]
    ways = [[(d, neighbour(d, turn)) for d in range(replicas)] for turn in (1, -1)]
    other = lax.ppermute(trade, "dp", partner)
    counts = counts.reshape(experts, 128)
    other_counts = lax.ppermute(counts, "dp", partner)

    def stage(body, offset, block, incoming, out_shape, out_spec, name):
        first, count = block

        def chunk(me):
            turn = offset * (1 - 2 * lax.rem(me[0], 2))
            return lax.rem(lax.div(me[0], 2) + turn + ring, ring)

        grads = pl.BlockSpec((count, slots, part), lambda i, me: (first, 0, 0))
        specs = [
            pl.BlockSpec((experts, 128), lambda i, me: (0, 0)),
            pl.BlockSpec((experts, 128), lambda i, me: (0, 0)),
            pl.BlockSpec((slots, part), lambda i, me: (0, 2 * chunk(me) + lax.rem(me[0], 2))),
            pl.BlockSpec((1, slots, part), lambda i, me: (tiles + chunk(me), 0, 0)),
            grads,
            grads,
        ]
        specs += [pl.BlockSpec(a.shape, lambda i, me: (0, 0)) for a in incoming]
        return call(
            body,
            grid_spec=pltpu.PrefetchScalarGridSpec(
                num_scalar_prefetch=1, grid=(1,), in_specs=specs, out_specs=out_spec
            ),
            out_shape=out_shape,
            cost_estimate=cost(
                4 * part * slots * count * part, 4 * slots * count * part + 4 * part * wide
            ),
            name=name,
        )(me, counts, other_counts, rows, other, trade, other, *incoming)

    def flat(columns):
        return sds((part, columns), BF16), pl.BlockSpec((part, columns), lambda i, me: (0, 0))

    state = [None, None]
    for step in range(ring // 2):
        k = ring // 2 - step
        for side in range(2):
            if step == 0:
                block = (side, tiles // 2)
                send = stage(first_kernel, k, block, [], *flat(wide // 2), f"ring_{step}_{side}")
            else:
                body = functools.partial(second_kernel, side) if step == 1 else middle_kernel
                offset = k if side == 0 else -k
                send = stage(
                    body, offset, (0, tiles), [state[side]], *flat(wide), f"ring_{step}_{side}"
                )
            state[side] = lax.ppermute(send, "dp", ways[side])
    weight_grad = stage(
        functools.partial(last_kernel, replicas),
        0,
        (0, tiles),
        state,
        sds((part, 1, wide), F32),
        pl.BlockSpec((part, 1, wide), lambda i, me: (0, 0, 0)),
        "ring_last",
    )

    spread = call(
        spread_kernel,
        out_shape=sds((2, 2 * tokens, experts * 8), BF16),
        cost_estimate=cost(experts * 64 * pairs * tokens, 128 * experts * tokens),
        name="spread",
    )(target, weights.reshape(tokens, chosen).T)
    input_grad = call(
        combine_kernel,
        out_shape=sds((tokens, model), BF16),
        cost_estimate=cost(8 * tokens * experts * 8 * model, 2 * slots * model),
        name="combine",
    )(spread, returned.reshape(experts * 8, half))
    return input_grad.reshape(1, tokens, model), weight_grad


def solution(mesh):
    in_specs = (
        P("dp", "ep", None),
        P("dp", "ep", None),
        P("dp", "ep", None, None),
        P("dp", "ep", None, None),
        P("dp", "ep", None, None),
        P("ep", None, None),
    )
    out_specs = (P("dp", "ep", None), P("dp", "ep", None))

    return jax.shard_map(shards, mesh=mesh, in_specs=in_specs, out_specs=out_specs, check_vma=False)
```

```python
import functools
import jax
import jax.numpy as jnp
from jax import lax
from jax.experimental import pallas as pl
from jax.experimental.pallas import tpu as pltpu
from jax.sharding import PartitionSpec as P

ROWS_LIMIT = 60 << 20
BF16, F32, I32 = jnp.bfloat16, jnp.float32, jnp.int32


def dot(a, b, ca, cb):
    return lax.dot_general(a, b, (((ca,), (cb,)), ((), ())), preferred_element_type=F32)


def iota(shape, dim):
    return lax.broadcasted_iota(I32, shape, dim)


def cost(flops, nbytes):
    return pl.CostEstimate(flops=flops, bytes_accessed=nbytes, transcendentals=0)


def flatten_pairs(x_t):
    chosen, tokens = x_t.shape
    pairs = chosen * tokens
    pair = iota((chosen, pairs), 1)
    mine = pair % chosen == iota((chosen, pairs), 0)
    out = jnp.zeros((chosen, pairs), x_t.dtype)
    for t in range(tokens):
        out = jnp.where(mine & (pair // chosen == t), x_t[:, t : t + 1], out)
    return jnp.sum(out, axis=0, keepdims=True)


def route_kernel(ids_ref, cnt_ref, tgt_ref):
    experts = cnt_ref.shape[0]
    flat = flatten_pairs(ids_ref[...])
    pairs = flat.shape[1]
    onehot = (iota((experts, pairs), 0) == flat).astype(F32)
    upper = (iota((pairs, pairs), 0) < iota((pairs, pairs), 1)).astype(BF16)
    before = dot(onehot.astype(BF16), upper, 1, 0)
    rank = jnp.sum(before * onehot, axis=0, keepdims=True).astype(I32)
    tgt_ref[...] = flat * 8 + rank
    counts = jnp.sum(onehot, axis=1, keepdims=True).astype(I32)
    cnt_ref[:, 0, :] = jnp.broadcast_to(counts, (experts, cnt_ref.shape[2]))


def rows_kernel(me_ref, gu_ref, hg_ref, rows_ref, wlo_ref, whi_ref, trade_ref, mine_ref, out_ref, grads_ref):
    @pl.when(pl.program_id(0) == 0)
    def _():
        hidden = hg_ref.shape[1]
        gate = gu_ref[:, :hidden].astype(F32)
        up = gu_ref[:, hidden:].astype(F32)
        grad = hg_ref[...].astype(F32)
        sigma = jax.nn.sigmoid(gate)
        grads_ref[:, :hidden] = (grad * up * sigma * (1.0 + gate * (1.0 - sigma))).astype(BF16)
        grads_ref[:, hidden:] = (grad * gate * sigma).astype(BF16)
        part = trade_ref.shape[2]
        tiles = 2 * hidden // part
        for tile in range(tiles):
            trade_ref[tile] = grads_ref[:, tile * part : (tile + 1) * part]
        second = lax.rem(me_ref[0], 2) == 0
        for chunk in range(trade_ref.shape[0] - tiles):
            start = 2 * chunk * part
            even = rows_ref[:, start : start + part]
            odd = rows_ref[:, start + part : start + 2 * part]
            trade_ref[tiles + chunk] = jnp.where(second, odd, even)
            mine_ref[chunk] = jnp.where(second, even, odd)

    grads = grads_ref[...]
    low = dot(grads, wlo_ref[...], 1, 1)
    high = dot(grads, whi_ref[...], 1, 1)
    slots, width = low.shape
    low = low.reshape(slots // 8, 8, width)
    high = high.reshape(slots // 8, 8, width)
    first = iota(low.shape, 1) < 4
    out_ref[:, 0] = jnp.where(first, low, pltpu.roll(high, 4, 1)).astype(BF16)
    out_ref[:, 1] = jnp.where(first, pltpu.roll(low, 4, 1), high).astype(BF16)


def live(cnt_ref, slots, part):
    experts = cnt_ref.shape[0]
    spread = (iota((slots, experts), 0) // 4 == iota((slots, experts), 1)).astype(BF16)
    counts = dot(spread, cnt_ref[...].astype(F32).astype(BF16), 1, 0)
    mask = (iota((slots, counts.shape[1]), 0) % 4).astype(F32) < counts
    return mask[:, :part]


def tiles_of(ref):
    return jnp.concatenate([ref[tile] for tile in range(ref.shape[0])], axis=1)


def partial_sum(cnt_a, cnt_b, rows_a, rows_b, grads_a, grads_b):
    slots, part = rows_a.shape[1:]
    zero = jnp.zeros((), F32)
    a = jnp.where(live(cnt_a, slots, part), rows_a[0].astype(F32), zero).astype(BF16)
    b = jnp.where(live(cnt_b, slots, part), rows_b[0].astype(F32), zero).astype(BF16)
    return dot(a, tiles_of(grads_a), 0, 0) + dot(b, tiles_of(grads_b), 0, 0)


def first_kernel(me_ref, *refs):
    refs[-1][...] = partial_sum(*refs[:6]).astype(BF16)


def second_kernel(side, me_ref, *refs):
    inc, out_ref = refs[6:]
    half = inc.shape[1]
    total = partial_sum(*refs[:6])
    low, high = total[:, :half], total[:, half:]
    if side == 0:
        low = low + inc[...].astype(F32)
    else:
        high = high + inc[...].astype(F32)
    out_ref[:, :half] = low.astype(BF16)
    out_ref[:, half:] = high.astype(BF16)


def middle_kernel(me_ref, *refs):
    inc, out_ref = refs[6:]
    out_ref[...] = (partial_sum(*refs[:6]) + inc[...].astype(F32)).astype(BF16)


def own_kernel(me_ref, *refs):
    refs[-1][...] = partial_sum(*refs[:6])


def last_kernel(replicas, own_ref, one_ref, two_ref, out_ref):
    total = own_ref[...] + (one_ref[...].astype(F32) + two_ref[...].astype(F32))
    out_ref[:, 0, :] = total / replicas


def spread_kernel(tgt_ref, w_ref, out_ref):
    _, double, rows = out_ref.shape
    tokens = double // 2
    pairs = tgt_ref.shape[1]
    chosen = pairs // tokens
    weight = flatten_pairs(w_ref[...])
    token_of = (iota((tokens, pairs), 1) // chosen == iota((tokens, pairs), 0)).astype(BF16)
    for side in range(2):
        hit = iota((rows, pairs), 0) == tgt_ref[...] + 4 * side
        spread = jnp.where(hit, weight, jnp.zeros((), F32))
        high = spread.astype(BF16)
        low = (spread - high.astype(F32)).astype(BF16)
        out_ref[side, :tokens] = dot(token_of, high, 1, 1).astype(BF16)
        out_ref[side, tokens:] = dot(token_of, low, 1, 1).astype(BF16)


def combine_kernel(spread_ref, recv_ref, out_ref):
    tokens, model = out_ref.shape
    recv = recv_ref[...]
    for side in range(2):
        both = dot(spread_ref[side], recv, 1, 0)
        out = both[:tokens] + both[tokens:]
        out_ref[:, side * (model // 2) : (side + 1) * (model // 2)] = out.astype(BF16)


def shards(ids, weights, rows, gate_up, hidden_grad, expert_weight, interpret=False):
    def call(body, limit=16 << 20, **options):
        params = pltpu.CompilerParams(vmem_limit_bytes=limit)
        return pl.pallas_call(body, interpret=interpret, compiler_params=params, **options)

    tokens, chosen = ids.shape[1:]
    slots, model = rows.shape[2:]
    hidden = hidden_grad.shape[3]
    wide = 2 * hidden
    experts = lax.axis_size("ep")
    replicas = lax.axis_size("dp")
    ring = replicas // 2
    part = model // replicas
    pairs = tokens * chosen
    rows = rows.reshape(slots, model)
    gate_up = gate_up.reshape(slots, wide)
    hidden_grad = hidden_grad.reshape(slots, hidden)
    expert_weight = expert_weight.reshape(model, wide)
    me = lax.axis_index("dp").astype(I32).reshape(1)
    sds = jax.ShapeDtypeStruct

    counts, target = call(
        route_kernel,
        limit=60 << 20,
        out_shape=(sds((experts, 1, 128), I32), sds((1, pairs), I32)),
        name="route",
    )(ids.reshape(tokens, chosen).T)
    counts = lax.all_to_all(counts, "ep", split_axis=0, concat_axis=0, tiled=True)

    half = model // 2
    tile = min(256, half)
    steps = half // tile
    tiles = wide // part
    trade, mine, sent = call(
        rows_kernel,
        limit=ROWS_LIMIT,
        grid_spec=pltpu.PrefetchScalarGridSpec(
            num_scalar_prefetch=1,
            grid=(steps,),
            in_specs=[
                pl.BlockSpec((slots, wide), lambda i, me: (0, 0)),
                pl.BlockSpec((slots, hidden), lambda i, me: (0, 0)),
                pl.BlockSpec((slots, model), lambda i, me: (0, 0)),
                pl.BlockSpec((tile, wide), lambda i, me: (i, 0)),
                pl.BlockSpec((tile, wide), lambda i, me: (i + steps, 0)),
            ],
            out_specs=(
                pl.BlockSpec((tiles + ring, slots, part), lambda i, me: (0, 0, 0)),
                pl.BlockSpec((ring, slots, part), lambda i, me: (0, 0, 0)),
                pl.BlockSpec((slots // 8, 2, 8, tile), lambda i, me: (0, 0, 0, i)),
            ),
            scratch_shapes=[pltpu.VMEM((slots, wide), BF16)],
        ),
        out_shape=(
            sds((tiles + ring, slots, part), BF16),
            sds((ring, slots, part), BF16),
            sds((slots // 8, 2, 8, half), BF16),
        ),
        cost_estimate=cost(2 * slots * model * wide, 2 * (model * wide + 4 * slots * wide)),
        name="rows",
    )(me, gate_up, hidden_grad, rows, expert_weight, expert_weight)
    returned = lax.all_to_all(
        sent.reshape(experts, 8, half), "ep", split_axis=0, concat_axis=0, tiled=True
    )

    def neighbour(d, direction):
        turn = direction if d % 2 == 0 else -direction
        return ((d // 2 + turn) % ring) * 2 + d % 2

    partner = [(d, d ^ 1) for d in range(replicas)]
    ways = [[(d, neighbour(d, turn)) for d in range(replicas)] for turn in (1, -1)]
    other = lax.ppermute(trade, "dp", partner)
    counts = counts.reshape(experts, 128)
    other_counts = lax.ppermute(counts, "dp", partner)

    def stage(body, offset, block, incoming, out_shape, out_spec, name):
        first, count = block

        def chunk(me):
            turn = offset * (1 - 2 * lax.rem(me[0], 2))
            return lax.rem(lax.div(me[0], 2) + turn + ring, ring)

        grads = pl.BlockSpec((count, slots, part), lambda i, me: (first, 0, 0))
        specs = [
            pl.BlockSpec((experts, 128), lambda i, me: (0, 0)),
            pl.BlockSpec((experts, 128), lambda i, me: (0, 0)),
            pl.BlockSpec((1, slots, part), lambda i, me: (chunk(me), 0, 0)),
            pl.BlockSpec((1, slots, part), lambda i, me: (tiles + chunk(me), 0, 0)),
            grads,
            grads,
        ]
        specs += [pl.BlockSpec(a.shape, lambda i, me: (0, 0)) for a in incoming]
        return call(
            body,
            grid_spec=pltpu.PrefetchScalarGridSpec(
                num_scalar_prefetch=1, grid=(1,), in_specs=specs, out_specs=out_spec
            ),
            out_shape=out_shape,
            cost_estimate=cost(
                4 * part * slots * count * part, 4 * slots * count * part + 4 * part * wide
            ),
            name=name,
        )(me, counts, other_counts, mine, other, trade, other, *incoming)

    def flat(columns):
        return sds((part, columns), BF16), pl.BlockSpec((part, columns), lambda i, me: (0, 0))

    own = stage(
        own_kernel,
        0,
        (0, tiles),
        [],
        sds((part, wide), F32),
        pl.BlockSpec((part, wide), lambda i, me: (0, 0)),
        "own",
    )
    state = [None, None]
    for step in range(ring // 2):
        k = ring // 2 - step
        for side in range(2):
            if step == 0:
                block = (side, tiles // 2)
                send = stage(first_kernel, k, block, [], *flat(wide // 2), f"ring_{step}_{side}")
            else:
                body = functools.partial(second_kernel, side) if step == 1 else middle_kernel
                offset = k if side == 0 else -k
                send = stage(
                    body, offset, (0, tiles), [state[side]], *flat(wide), f"ring_{step}_{side}"
                )
            state[side] = lax.ppermute(send, "dp", ways[side])
    weight_grad = call(
        functools.partial(last_kernel, replicas),
        out_shape=sds((part, 1, wide), F32),
        cost_estimate=cost(3 * part * wide, 12 * part * wide),
        name="ring_last",
    )(own, *state)

    spread = call(
        spread_kernel,
        out_shape=sds((2, 2 * tokens, experts * 8), BF16),
        cost_estimate=cost(experts * 64 * pairs * tokens, 128 * experts * tokens),
        name="spread",
    )(target, weights.reshape(tokens, chosen).T)
    input_grad = call(
        combine_kernel,
        out_shape=sds((tokens, model), BF16),
        cost_estimate=cost(8 * tokens * experts * 8 * model, 2 * slots * model),
        name="combine",
    )(spread, returned.reshape(experts * 8, half))
    return input_grad.reshape(1, tokens, model), weight_grad


def solution(mesh):
    in_specs = (
        P("dp", "ep", None),
        P("dp", "ep", None),
        P("dp", "ep", None, None),
        P("dp", "ep", None, None),
        P("dp", "ep", None, None),
        P("ep", None, None),
    )
    out_specs = (P("dp", "ep", None), P("dp", "ep", None))

    return jax.shard_map(shards, mesh=mesh, in_specs=in_specs, out_specs=out_specs, check_vma=False)
```

```python
import functools
import jax
import jax.numpy as jnp
from jax import lax
from jax.experimental import pallas as pl
from jax.experimental.pallas import tpu as pltpu
from jax.sharding import PartitionSpec as P

ROWS_LIMIT = 60 << 20
CHAINS = 2
BF16, F32, I32 = jnp.bfloat16, jnp.float32, jnp.int32


def dot(a, b, ca, cb):
    return lax.dot_general(a, b, (((ca,), (cb,)), ((), ())), preferred_element_type=F32)


def iota(shape, dim):
    return lax.broadcasted_iota(I32, shape, dim)


def cost(flops, nbytes):
    return pl.CostEstimate(flops=flops, bytes_accessed=nbytes, transcendentals=0)


def flatten_pairs(x_t):
    chosen, tokens = x_t.shape
    pairs = chosen * tokens
    pair = iota((chosen, pairs), 1)
    mine = pair % chosen == iota((chosen, pairs), 0)
    out = jnp.zeros((chosen, pairs), x_t.dtype)
    for t in range(tokens):
        out = jnp.where(mine & (pair // chosen == t), x_t[:, t : t + 1], out)
    return jnp.sum(out, axis=0, keepdims=True)


def route_kernel(ids_ref, cnt_ref, tgt_ref):
    experts = cnt_ref.shape[0]
    flat = flatten_pairs(ids_ref[...])
    pairs = flat.shape[1]
    onehot = (iota((experts, pairs), 0) == flat).astype(F32)
    upper = (iota((pairs, pairs), 0) < iota((pairs, pairs), 1)).astype(BF16)
    before = dot(onehot.astype(BF16), upper, 1, 0)
    rank = jnp.sum(before * onehot, axis=0, keepdims=True).astype(I32)
    tgt_ref[...] = flat * 8 + rank
    counts = jnp.sum(onehot, axis=1, keepdims=True).astype(I32)
    cnt_ref[:, 0, :] = jnp.broadcast_to(counts, (experts, cnt_ref.shape[2]))


def rows_kernel(me_ref, gu_ref, hg_ref, rows_ref, wlo_ref, whi_ref, trade_ref, mine_ref, out_ref, grads_ref):
    @pl.when(pl.program_id(0) == 0)
    def _():
        hidden = hg_ref.shape[1]
        gate = gu_ref[:, :hidden].astype(F32)
        up = gu_ref[:, hidden:].astype(F32)
        grad = hg_ref[...].astype(F32)
        sigma = jax.nn.sigmoid(gate)
        grads_ref[:, :hidden] = (grad * up * sigma * (1.0 + gate * (1.0 - sigma))).astype(BF16)
        grads_ref[:, hidden:] = (grad * gate * sigma).astype(BF16)
        part = trade_ref.shape[2]
        tiles = 2 * hidden // part
        for tile in range(tiles):
            trade_ref[tile] = grads_ref[:, tile * part : (tile + 1) * part]
        ring = mine_ref.shape[0]
        core, chip = lax.rem(me_ref[0], 2), lax.div(me_ref[0], 2)
        for owner, ref, base in ((core, mine_ref, 0), (1 - core, trade_ref, tiles)):
            for index in range(ring):
                k = index // 2 + 1 if index < ring - 2 else (ring // 2, 0)[index - ring + 2]
                dest = lax.rem(chip + k * (1 - 2 * owner) + ring, ring)
                row_set = index % 2 if index < ring - 2 else owner
                start = pl.multiple_of((2 * dest + row_set) * part, part)
                ref[base + index] = rows_ref[:, pl.ds(start, part)]

    grads = grads_ref[...]
    low = dot(grads, wlo_ref[...], 1, 1)
    high = dot(grads, whi_ref[...], 1, 1)
    slots, width = low.shape
    low = low.reshape(slots // 8, 8, width)
    high = high.reshape(slots // 8, 8, width)
    first = iota(low.shape, 1) < 4
    out_ref[:, 0] = jnp.where(first, low, pltpu.roll(high, 4, 1)).astype(BF16)
    out_ref[:, 1] = jnp.where(first, pltpu.roll(low, 4, 1), high).astype(BF16)


def live(cnt_ref, slots, part):
    experts = cnt_ref.shape[0]
    spread = (iota((slots, experts), 0) // 4 == iota((slots, experts), 1)).astype(BF16)
    counts = dot(spread, cnt_ref[...].astype(F32).astype(BF16), 1, 0)
    mask = (iota((slots, counts.shape[1]), 0) % 4).astype(F32) < counts
    return mask[:, :part]


def tiles_of(ref):
    return jnp.concatenate([ref[tile] for tile in range(ref.shape[0])], axis=1)


def masked(cnt_ref, tile, slots, part):
    return jnp.where(live(cnt_ref, slots, part), tile.astype(F32), jnp.zeros((), F32)).astype(BF16)


def tile_sums(cnt_a, cnt_b, rows_a, rows_b, grads_a, grads_b):
    count, slots, part = rows_a.shape
    one, two = tiles_of(grads_a), tiles_of(grads_b)
    return [
        dot(masked(cnt_a, rows_a[t], slots, part), one, 0, 0)
        + dot(masked(cnt_b, rows_b[t], slots, part), two, 0, 0)
        for t in range(count)
    ]


def first_kernel(me_ref, *refs):
    refs[-1][...] = tile_sums(*refs[:6])[0].astype(BF16)


def second_kernel(me_ref, *refs):
    inc_ref, out_ref = refs[6:]
    core = lax.rem(me_ref[0], 2)
    inc = inc_ref[...].astype(F32)
    for t, total in enumerate(tile_sums(*refs[:6])):
        out_ref[t] = (total + jnp.where(core == t, inc, jnp.zeros((), F32))).astype(BF16)


def middle_kernel(me_ref, *refs):
    inc_ref, out_ref = refs[6:]
    for t, total in enumerate(tile_sums(*refs[:6])):
        out_ref[t] = (total + inc_ref[t].astype(F32)).astype(BF16)


def final_kernel(me_ref, *refs):
    inc_ref, same_ref, cross_ref = refs[6:]
    low, high = [
        total + inc_ref[t].astype(F32) for t, total in enumerate(tile_sums(*refs[:6]))
    ]
    even = lax.rem(me_ref[0], 2) == 0
    same_ref[...] = jnp.where(even, low, high).astype(BF16)
    cross_ref[...] = jnp.where(even, high, low).astype(BF16)


def own_kernel(me_ref, *refs):
    refs[-1][...] = tile_sums(*refs[:6])[0]


def last_kernel(replicas, own_ref, *refs):
    out_ref = refs[-1]
    width = refs[0].shape[1]
    for q in range(CHAINS):
        cols = slice(q * width, (q + 1) * width)
        arrived = refs[2 * q][...].astype(F32) + refs[2 * q + 1][...].astype(F32)
        out_ref[:, 0, cols] = (own_ref[:, cols] + arrived) / replicas


def spread_kernel(tgt_ref, w_ref, out_ref):
    _, double, rows = out_ref.shape
    tokens = double // 2
    pairs = tgt_ref.shape[1]
    chosen = pairs // tokens
    weight = flatten_pairs(w_ref[...])
    token_of = (iota((tokens, pairs), 1) // chosen == iota((tokens, pairs), 0)).astype(BF16)
    for side in range(2):
        hit = iota((rows, pairs), 0) == tgt_ref[...] + 4 * side
        spread = jnp.where(hit, weight, jnp.zeros((), F32))
        high = spread.astype(BF16)
        low = (spread - high.astype(F32)).astype(BF16)
        out_ref[side, :tokens] = dot(token_of, high, 1, 1).astype(BF16)
        out_ref[side, tokens:] = dot(token_of, low, 1, 1).astype(BF16)


def combine_kernel(spread_ref, recv_ref, out_ref):
    tokens, model = out_ref.shape
    recv = recv_ref[...]
    width = recv.shape[1]
    for side in range(2):
        both = dot(spread_ref[side], recv, 1, 0)
        out = both[:tokens] + both[tokens:]
        start = pl.multiple_of(side * (model // 2) + pl.program_id(0) * width, width)
        out_ref[:, pl.ds(start, width)] = out.astype(BF16)


def shards(ids, weights, rows, gate_up, hidden_grad, expert_weight, interpret=False):
    def call(body, limit=16 << 20, **options):
        params = pltpu.CompilerParams(vmem_limit_bytes=limit)
        return pl.pallas_call(body, interpret=interpret, compiler_params=params, **options)

    tokens, chosen = ids.shape[1:]
    slots, model = rows.shape[2:]
    hidden = hidden_grad.shape[3]
    wide = 2 * hidden
    experts = lax.axis_size("ep")
    replicas = lax.axis_size("dp")
    ring = replicas // 2
    part = model // replicas
    pairs = tokens * chosen
    rows = rows.reshape(slots, model)
    gate_up = gate_up.reshape(slots, wide)
    hidden_grad = hidden_grad.reshape(slots, hidden)
    expert_weight = expert_weight.reshape(model, wide)
    me = lax.axis_index("dp").astype(I32).reshape(1)
    sds = jax.ShapeDtypeStruct

    counts, target = call(
        route_kernel,
        limit=60 << 20,
        out_shape=(sds((experts, 1, 128), I32), sds((1, pairs), I32)),
        name="route",
    )(ids.reshape(tokens, chosen).T)
    counts = lax.all_to_all(counts, "ep", split_axis=0, concat_axis=0, tiled=True)

    half = model // 2
    tile = min(256, half)
    steps = half // tile
    tiles = wide // part
    trade, mine, sent = call(
        rows_kernel,
        limit=ROWS_LIMIT,
        grid_spec=pltpu.PrefetchScalarGridSpec(
            num_scalar_prefetch=1,
            grid=(steps,),
            in_specs=[
                pl.BlockSpec((slots, wide), lambda i, me: (0, 0)),
                pl.BlockSpec((slots, hidden), lambda i, me: (0, 0)),
                pl.BlockSpec((slots, model), lambda i, me: (0, 0)),
                pl.BlockSpec((tile, wide), lambda i, me: (i, 0)),
                pl.BlockSpec((tile, wide), lambda i, me: (i + steps, 0)),
            ],
            out_specs=(
                pl.BlockSpec((tiles + ring, slots, part), lambda i, me: (0, 0, 0)),
                pl.BlockSpec((ring, slots, part), lambda i, me: (0, 0, 0)),
                pl.BlockSpec((slots // 8, 2, 8, tile), lambda i, me: (0, 0, 0, i)),
            ),
            scratch_shapes=[pltpu.VMEM((slots, wide), BF16)],
        ),
        out_shape=(
            sds((tiles + ring, slots, part), BF16),
            sds((ring, slots, part), BF16),
            sds((slots // 8, 2, 8, half), BF16),
        ),
        cost_estimate=cost(2 * slots * model * wide, 2 * (model * wide + 4 * slots * wide)),
        name="rows",
    )(me, gate_up, hidden_grad, rows, expert_weight, expert_weight)
    returned = lax.all_to_all(
        sent.reshape(experts, 8, half), "ep", split_axis=0, concat_axis=0, tiled=True
    )

    def onward(d, cross):
        core = d % 2
        return ((d // 2 + 1 - 2 * core) % ring) * 2 + (1 - core if cross else core)

    partner = [(d, d ^ 1) for d in range(replicas)]
    ways = [[(d, onward(d, cross)) for d in range(replicas)] for cross in (False, True)]
    other = lax.ppermute(trade, "dp", partner)
    counts = counts.reshape(experts, 128)
    other_counts = lax.ppermute(counts, "dp", partner)

    width = wide // CHAINS

    def stage(body, first, count, chain, chains, incoming, out_shapes, name):
        grads = pl.BlockSpec((tiles // chains, slots, part), lambda i, me: (chain, 0, 0))
        specs = [
            pl.BlockSpec((experts, 128), lambda i, me: (0, 0)),
            pl.BlockSpec((experts, 128), lambda i, me: (0, 0)),
            pl.BlockSpec((count, slots, part), lambda i, me: (first // count, 0, 0)),
            pl.BlockSpec((count, slots, part), lambda i, me: ((tiles + first) // count, 0, 0)),
            grads,
            grads,
        ]
        block = lambda a: pl.BlockSpec(a.shape, lambda i, me: (0,) * len(a.shape))
        return call(
            body,
            grid_spec=pltpu.PrefetchScalarGridSpec(
                num_scalar_prefetch=1,
                grid=(1,),
                in_specs=specs + [block(a) for a in incoming],
                out_specs=[block(a) for a in out_shapes],
            ),
            out_shape=out_shapes,
            cost_estimate=cost(
                4 * count * part * slots * wide // chains,
                4 * slots * wide // chains + 4 * part * wide,
            ),
            name=name,
        )(me, counts, other_counts, mine, other, trade, other, *incoming)

    own = stage(own_kernel, ring - 1, 1, 0, 1, [], [sds((part, wide), F32)], "own")
    one, two = sds((part, width), BF16), sds((2, part, width), BF16)
    state = [[]] * CHAINS
    for step in range(ring // 2):
        first, count = (ring - 2, 1) if step == 0 else (ring - 2 - 2 * step, 2)
        final = step == ring // 2 - 1
        body = (first_kernel, second_kernel, middle_kernel)[min(step, 2)]
        for chain in range(CHAINS):
            sends = stage(
                final_kernel if final else body,
                first,
                count,
                chain,
                CHAINS,
                state[chain],
                [one, one] if final else [one if step == 0 else two],
                f"ring_{step}_{chain}",
            )
            state[chain] = [lax.ppermute(a, "dp", way) for a, way in zip(sends, ways)]
    weight_grad = call(
        functools.partial(last_kernel, replicas),
        out_shape=sds((part, 1, wide), F32),
        cost_estimate=cost(3 * part * wide, 12 * part * wide),
        name="ring_last",
    )(own[0], *state[0], *state[1])

    spread = call(
        spread_kernel,
        out_shape=sds((2, 2 * tokens, experts * 8), BF16),
        cost_estimate=cost(experts * 64 * pairs * tokens, 128 * experts * tokens),
        name="spread",
    )(target, weights.reshape(tokens, chosen).T)
    input_grad = call(
        combine_kernel,
        grid=(steps,),
        in_specs=[
            pl.BlockSpec((2, 2 * tokens, experts * 8), lambda i: (0, 0, 0)),
            pl.BlockSpec((experts * 8, tile), lambda i: (0, i)),
        ],
        out_specs=pl.BlockSpec((tokens, model), lambda i: (0, 0)),
        out_shape=sds((tokens, model), BF16),
        cost_estimate=cost(8 * tokens * experts * 8 * model, 2 * slots * model),
        name="combine",
    )(spread, returned.reshape(experts * 8, half))
    return input_grad.reshape(1, tokens, model), weight_grad


def solution(mesh):
    in_specs = (
        P("dp", "ep", None),
        P("dp", "ep", None),
        P("dp", "ep", None, None),
        P("dp", "ep", None, None),
        P("dp", "ep", None, None),
        P("ep", None, None),
    )
    out_specs = (P("dp", "ep", None), P("dp", "ep", None))

    return jax.shard_map(shards, mesh=mesh, in_specs=in_specs, out_specs=out_specs, check_vma=False)
```

```python
import functools
import jax
import jax.numpy as jnp
from jax import lax
from jax.experimental import pallas as pl
from jax.experimental.pallas import tpu as pltpu
from jax.sharding import PartitionSpec as P

ROWS_LIMIT = 60 << 20
CHAINS = 2
BF16, F32, I32 = jnp.bfloat16, jnp.float32, jnp.int32


def dot(a, b, ca, cb):
    return lax.dot_general(a, b, (((ca,), (cb,)), ((), ())), preferred_element_type=F32)


def iota(shape, dim):
    return lax.broadcasted_iota(I32, shape, dim)


def cost(flops, nbytes):
    return pl.CostEstimate(flops=flops, bytes_accessed=nbytes, transcendentals=0)


def flatten_pairs(x_t):
    chosen, tokens = x_t.shape
    pairs = chosen * tokens
    pair = iota((chosen, pairs), 1)
    mine = pair % chosen == iota((chosen, pairs), 0)
    out = jnp.zeros((chosen, pairs), x_t.dtype)
    for t in range(tokens):
        out = jnp.where(mine & (pair // chosen == t), x_t[:, t : t + 1], out)
    return jnp.sum(out, axis=0, keepdims=True)


def route_kernel(ids_ref, cnt_ref, tgt_ref):
    experts = cnt_ref.shape[0]
    flat = flatten_pairs(ids_ref[...])
    pairs = flat.shape[1]
    onehot = (iota((experts, pairs), 0) == flat).astype(F32)
    upper = (iota((pairs, pairs), 0) < iota((pairs, pairs), 1)).astype(BF16)
    before = dot(onehot.astype(BF16), upper, 1, 0)
    rank = jnp.sum(before * onehot, axis=0, keepdims=True).astype(I32)
    tgt_ref[...] = flat * 8 + rank
    counts = jnp.sum(onehot, axis=1, keepdims=True).astype(I32)
    cnt_ref[:, 0, :] = jnp.broadcast_to(counts, (experts, cnt_ref.shape[2]))


def rows_kernel(me_ref, gu_ref, hg_ref, rows_ref, wlo_ref, whi_ref, trade_ref, mine_ref, out_ref, grads_ref):
    @pl.when(pl.program_id(0) == 0)
    def _():
        hidden = hg_ref.shape[1]
        gate = gu_ref[:, :hidden].astype(F32)
        up = gu_ref[:, hidden:].astype(F32)
        grad = hg_ref[...].astype(F32)
        sigma = jax.nn.sigmoid(gate)
        grads_ref[:, :hidden] = (grad * up * sigma * (1.0 + gate * (1.0 - sigma))).astype(BF16)
        grads_ref[:, hidden:] = (grad * gate * sigma).astype(BF16)
        part = trade_ref.shape[2]
        tiles = 2 * hidden // part
        for tile in range(tiles):
            trade_ref[tile] = grads_ref[:, tile * part : (tile + 1) * part]
        ring = mine_ref.shape[0]
        core, chip = lax.rem(me_ref[0], 2), lax.div(me_ref[0], 2)
        for owner, ref, base in ((core, mine_ref, 0), (1 - core, trade_ref, tiles)):
            for index in range(ring):
                k = index // 2 + 1 if index < ring - 2 else (ring // 2, 0)[index - ring + 2]
                dest = lax.rem(chip + k * (1 - 2 * owner) + ring, ring)
                row_set = index % 2 if index < ring - 2 else owner
                start = pl.multiple_of((2 * dest + row_set) * part, part)
                ref[base + index] = rows_ref[:, pl.ds(start, part)]

    grads = grads_ref[...]
    low = dot(grads, wlo_ref[...], 1, 1)
    high = dot(grads, whi_ref[...], 1, 1)
    slots, width = low.shape
    low = low.reshape(slots // 8, 8, width)
    high = high.reshape(slots // 8, 8, width)
    first = iota(low.shape, 1) < 4
    out_ref[:, 0] = jnp.where(first, low, pltpu.roll(high, 4, 1)).astype(BF16)
    out_ref[:, 1] = jnp.where(first, pltpu.roll(low, 4, 1), high).astype(BF16)


def live(cnt_ref, slots, part):
    experts = cnt_ref.shape[0]
    spread = (iota((slots, experts), 0) // 4 == iota((slots, experts), 1)).astype(BF16)
    counts = dot(spread, cnt_ref[...].astype(F32).astype(BF16), 1, 0)
    mask = (iota((slots, counts.shape[1]), 0) % 4).astype(F32) < counts
    return mask[:, :part]


def tiles_of(ref):
    return jnp.concatenate([ref[tile] for tile in range(ref.shape[0])], axis=1)


def masked(cnt_ref, tile, slots, part):
    return jnp.where(live(cnt_ref, slots, part), tile.astype(F32), jnp.zeros((), F32)).astype(BF16)


def tile_sums(cnt_a, cnt_b, rows_a, rows_b, grads_a, grads_b):
    count, slots, part = rows_a.shape
    one, two = tiles_of(grads_a), tiles_of(grads_b)
    return [
        dot(masked(cnt_a, rows_a[t], slots, part), one, 0, 0)
        + dot(masked(cnt_b, rows_b[t], slots, part), two, 0, 0)
        for t in range(count)
    ]


def first_kernel(me_ref, *refs):
    refs[-1][...] = tile_sums(*refs[:6])[0].astype(BF16)


def second_kernel(me_ref, *refs):
    inc_ref, out_ref = refs[6:]
    core = lax.rem(me_ref[0], 2)
    inc = inc_ref[...].astype(F32)
    for t, total in enumerate(tile_sums(*refs[:6])):
        out_ref[t] = (total + jnp.where(core == t, inc, jnp.zeros((), F32))).astype(BF16)


def middle_kernel(me_ref, *refs):
    inc_ref, out_ref = refs[6:]
    for t, total in enumerate(tile_sums(*refs[:6])):
        out_ref[t] = (total + inc_ref[t].astype(F32)).astype(BF16)


def final_kernel(me_ref, *refs):
    inc_ref, same_ref, cross_ref = refs[6:]
    low, high = [
        total + inc_ref[t].astype(F32) for t, total in enumerate(tile_sums(*refs[:6]))
    ]
    even = lax.rem(me_ref[0], 2) == 0
    same_ref[...] = jnp.where(even, low, high).astype(BF16)
    cross_ref[...] = jnp.where(even, high, low).astype(BF16)


def own_kernel(me_ref, *refs):
    refs[-1][...] = tile_sums(*refs[:6])[0]


def last_kernel(replicas, own_ref, *refs):
    out_ref = refs[-1]
    width = refs[0].shape[1]
    for q in range(CHAINS):
        cols = slice(q * width, (q + 1) * width)
        arrived = refs[2 * q][...].astype(F32) + refs[2 * q + 1][...].astype(F32)
        out_ref[:, 0, cols] = (own_ref[:, cols] + arrived) / replicas


def spread_kernel(tgt_ref, w_ref, out_ref):
    _, double, rows = out_ref.shape
    tokens = double // 2
    pairs = tgt_ref.shape[1]
    chosen = pairs // tokens
    weight = flatten_pairs(w_ref[...])
    token_of = (iota((tokens, pairs), 1) // chosen == iota((tokens, pairs), 0)).astype(BF16)
    for side in range(2):
        hit = iota((rows, pairs), 0) == tgt_ref[...] + 4 * side
        spread = jnp.where(hit, weight, jnp.zeros((), F32))
        high = spread.astype(BF16)
        low = (spread - high.astype(F32)).astype(BF16)
        out_ref[side, :tokens] = dot(token_of, high, 1, 1).astype(BF16)
        out_ref[side, tokens:] = dot(token_of, low, 1, 1).astype(BF16)


def combine_kernel(spread_ref, recv_ref, out_ref):
    tokens, model = out_ref.shape
    recv = recv_ref[...]
    for side in range(2):
        both = dot(spread_ref[side], recv, 1, 0)
        out = both[:tokens] + both[tokens:]
        out_ref[:, side * (model // 2) : (side + 1) * (model // 2)] = out.astype(BF16)


def shards(ids, weights, rows, gate_up, hidden_grad, expert_weight, interpret=False):
    def call(body, limit=16 << 20, **options):
        params = pltpu.CompilerParams(vmem_limit_bytes=limit)
        return pl.pallas_call(body, interpret=interpret, compiler_params=params, **options)

    tokens, chosen = ids.shape[1:]
    slots, model = rows.shape[2:]
    hidden = hidden_grad.shape[3]
    wide = 2 * hidden
    experts = lax.axis_size("ep")
    replicas = lax.axis_size("dp")
    ring = replicas // 2
    part = model // replicas
    pairs = tokens * chosen
    rows = rows.reshape(slots, model)
    gate_up = gate_up.reshape(slots, wide)
    hidden_grad = hidden_grad.reshape(slots, hidden)
    expert_weight = expert_weight.reshape(model, wide)
    me = lax.axis_index("dp").astype(I32).reshape(1)
    sds = jax.ShapeDtypeStruct

    counts, target = call(
        route_kernel,
        limit=60 << 20,
        out_shape=(sds((experts, 1, 128), I32), sds((1, pairs), I32)),
        name="route",
    )(ids.reshape(tokens, chosen).T)
    counts = lax.all_to_all(counts, "ep", split_axis=0, concat_axis=0, tiled=True)

    half = model // 2
    tile = min(256, half)
    steps = half // tile
    tiles = wide // part
    trade, mine, sent = call(
        rows_kernel,
        limit=ROWS_LIMIT,
        grid_spec=pltpu.PrefetchScalarGridSpec(
            num_scalar_prefetch=1,
            grid=(steps,),
            in_specs=[
                pl.BlockSpec((slots, wide), lambda i, me: (0, 0)),
                pl.BlockSpec((slots, hidden), lambda i, me: (0, 0)),
                pl.BlockSpec((slots, model), lambda i, me: (0, 0)),
                pl.BlockSpec((tile, wide), lambda i, me: (i, 0)),
                pl.BlockSpec((tile, wide), lambda i, me: (i + steps, 0)),
            ],
            out_specs=(
                pl.BlockSpec((tiles + ring, slots, part), lambda i, me: (0, 0, 0)),
                pl.BlockSpec((ring, slots, part), lambda i, me: (0, 0, 0)),
                pl.BlockSpec((slots // 8, 2, 8, tile), lambda i, me: (0, 0, 0, i)),
            ),
            scratch_shapes=[pltpu.VMEM((slots, wide), BF16)],
        ),
        out_shape=(
            sds((tiles + ring, slots, part), BF16),
            sds((ring, slots, part), BF16),
            sds((slots // 8, 2, 8, half), BF16),
        ),
        cost_estimate=cost(2 * slots * model * wide, 2 * (model * wide + 4 * slots * wide)),
        name="rows",
    )(me, gate_up, hidden_grad, rows, expert_weight, expert_weight)
    returned = lax.all_to_all(
        sent.reshape(experts, 8, half), "ep", split_axis=0, concat_axis=0, tiled=True
    )

    def onward(d, cross):
        core = d % 2
        return ((d // 2 + 1 - 2 * core) % ring) * 2 + (1 - core if cross else core)

    partner = [(d, d ^ 1) for d in range(replicas)]
    ways = [[(d, onward(d, cross)) for d in range(replicas)] for cross in (False, True)]
    other = lax.ppermute(trade, "dp", partner)
    counts = counts.reshape(experts, 128)
    other_counts = lax.ppermute(counts, "dp", partner)

    width = wide // CHAINS

    def stage(body, first, count, chain, chains, incoming, out_shapes, name):
        grads = pl.BlockSpec((tiles // chains, slots, part), lambda i, me: (chain, 0, 0))
        specs = [
            pl.BlockSpec((experts, 128), lambda i, me: (0, 0)),
            pl.BlockSpec((experts, 128), lambda i, me: (0, 0)),
            pl.BlockSpec((count, slots, part), lambda i, me: (first // count, 0, 0)),
            pl.BlockSpec((count, slots, part), lambda i, me: ((tiles + first) // count, 0, 0)),
            grads,
            grads,
        ]
        block = lambda a: pl.BlockSpec(a.shape, lambda i, me: (0,) * len(a.shape))
        return call(
            body,
            grid_spec=pltpu.PrefetchScalarGridSpec(
                num_scalar_prefetch=1,
                grid=(1,),
                in_specs=specs + [block(a) for a in incoming],
                out_specs=[block(a) for a in out_shapes],
            ),
            out_shape=out_shapes,
            cost_estimate=cost(
                4 * count * part * slots * wide // chains,
                4 * slots * wide // chains + 4 * part * wide,
            ),
            name=name,
        )(me, counts, other_counts, mine, other, trade, other, *incoming)

    own = stage(own_kernel, ring - 1, 1, 0, 1, [], [sds((part, wide), F32)], "own")
    one, two = sds((part, width), BF16), sds((2, part, width), BF16)
    state = [[]] * CHAINS
    for step in range(ring // 2):
        first, count = (ring - 2, 1) if step == 0 else (ring - 2 - 2 * step, 2)
        final = step == ring // 2 - 1
        body = (first_kernel, second_kernel, middle_kernel)[min(step, 2)]
        for chain in range(CHAINS):
            sends = stage(
                final_kernel if final else body,
                first,
                count,
                chain,
                CHAINS,
                state[chain],
                [one, one] if final else [one if step == 0 else two],
                f"ring_{step}_{chain}",
            )
            state[chain] = [lax.ppermute(a, "dp", way) for a, way in zip(sends, ways)]
    weight_grad = call(
        functools.partial(last_kernel, replicas),
        out_shape=sds((part, 1, wide), F32),
        cost_estimate=cost(3 * part * wide, 12 * part * wide),
        name="ring_last",
    )(own[0], *state[0], *state[1])

    spread = call(
        spread_kernel,
        out_shape=sds((2, 2 * tokens, experts * 8), BF16),
        cost_estimate=cost(experts * 64 * pairs * tokens, 128 * experts * tokens),
        name="spread",
    )(target, weights.reshape(tokens, chosen).T)
    input_grad = call(
        combine_kernel,
        out_shape=sds((tokens, model), BF16),
        cost_estimate=cost(8 * tokens * experts * 8 * model, 2 * slots * model),
        name="combine",
    )(spread, returned.reshape(experts * 8, half))
    return input_grad.reshape(1, tokens, model), weight_grad


def solution(mesh):
    in_specs = (
        P("dp", "ep", None),
        P("dp", "ep", None),
        P("dp", "ep", None, None),
        P("dp", "ep", None, None),
        P("dp", "ep", None, None),
        P("ep", None, None),
    )
    out_specs = (P("dp", "ep", None), P("dp", "ep", None))

    return jax.shard_map(shards, mesh=mesh, in_specs=in_specs, out_specs=out_specs, check_vma=False)
```
